256 devices in a mesh: pt: 4 (over x_hi, core), ch: 64 (over y, z, x_lo).
Axes of the slice: x: 4 (x_hi: 2, x_lo: 2; x = x_hi * 2 + x_lo), y: 4, z: 8, core: 2. Of those that a mesh axis runs over, the one named last changes fastest.
Arguments:
- voltages: bfloat16 [4096, 2, 64, 2048], P(('pt', 'ch')), parts along dimension 0, may hold values from -6 to 6
- beam_delay: int32 [1024, 64], P('pt'), parts along dimension 0, may hold values from 0 to 4095
- bandpass: float32 [1024], P('ch'), may hold values from 0.4 to 6
- trial_delays: int32 [512, 1024], replicated, may hold values from 0 to 511, as said below
Outputs:
- dedispersed: bfloat16 [2048, 256, 512], P(('pt', 'ch')), parts along dimension 0
The draws below stay inside these ranges and needn't reach their ends.
There are 4 independent parts, one for each index of `pt`. The reference program is written for one: setup_inputs(seed, part) draws one part's arguments, and reference() takes and returns one part's arrays. A program takes and returns all parts, laid end to end along the dimension named above; an argument that names none is the same for every part. Nothing has to cross between parts.
Inputs may be any that keep to these rules, and one draw needn't show every extreme that they name: `trial_delays`: delays are counted in integrated samples.
All inputs are finite; a program needn't handle non-finite values.
Results may differ from the reference program's by a relative error of at most 0.0028.
The reference program's roundings to bfloat16 on the way count: a program that leaves them out, or rounds other values in their place, can miss the bound.
Values may be sent and summed in bfloat16 or wider, within the bound.
No kernel may reach another device: no remote copies, remote signals or barrier semaphores. Data moves between devices by JAX's collectives and lax.ppermute only.
A program may use at most 64 MiB of HBM per device.

```python
import math
import jax
import jax.numpy as jnp
from jax import lax

CHANNELS = 1024
ANTENNAS = 64
BEAMS = 256
NT = 512
INTEG = 4
TRIALS = 512
S_RAW = 2048
NF = 256


def draw_bandpass(key, part):
    rising = 3.0 ** (jnp.arange(CHANNELS, dtype=jnp.float32) / CHANNELS)
    rough = jnp.exp(jax.random.uniform(key, (CHANNELS,), jnp.float32, -math.log(2.0), math.log(2.0)))
    return rising * rough


def draw_trial_delays(key, part):
    measures = jax.random.randint(key, (TRIALS,), 0, NT, dtype=jnp.int32)
    measures = measures.at[0].set(0).at[TRIALS - 1].set(NT - 1)
    channels = jnp.arange(CHANNELS, dtype=jnp.int32)
    scaled = 2 ** 30
    sweep_curve = scaled // (channels + CHANNELS) ** 2 - scaled // (2 * CHANNELS) ** 2
    return measures[:, None] * sweep_curve[None, :] // sweep_curve[0]


def place_ends(drawn, own_key, least, high):
    dims = drawn.shape
    place = [jax.random.randint(jax.random.fold_in(own_key, axis), (), 0, dims[axis]) for axis in range(len(dims))]
    drawn = drawn.at[tuple(place)].set(least)
    longest = dims.index(max(dims))
    place[longest] = (place[longest] + 1) % dims[longest]
    return drawn.at[tuple(place)].set(high)


def block_levels(key, shape, cuts, least, top_value):
    factor_of = 1.0
    for axis_at, shards_of in cuts:
        draws = jax.random.uniform(jax.random.fold_in(jax.random.fold_in(key, 6), axis_at), (shards_of,), jnp.float32, least / len(cuts), top_value / len(cuts))
        factor_of = factor_of * jnp.repeat(jnp.exp(draws), shape[axis_at] // shards_of).reshape((-1,) + (1,) * (len(shape) - 1 - axis_at))
    return factor_of


def bell_draw(own_key, shape, scale, limit, split=(), kind=jnp.bfloat16):
    level = block_levels(own_key, shape, split, -0.22, 0.18) if split else 1.0
    drawn = jax.random.normal(own_key, shape, jnp.float32) * scale * level
    return jnp.minimum(jnp.maximum(drawn, -limit), limit).astype(kind)


def setup_inputs(seed: int = 0, part: int = 0) -> dict:
    key_list = jax.random.split(jax.random.key(seed), 5)
    part_keys = jax.random.split(jax.random.fold_in(key_list[4], part), 5)
    voltages = bell_draw(part_keys[0], (CHANNELS, 2, ANTENNAS, S_RAW), 1.0, 6.0, ((0, 64),))
    beam_delay = place_ends(jax.random.randint(part_keys[1], (BEAMS, ANTENNAS), 0, 4096), jax.random.fold_in(part_keys[1], 1), 0, 4095).astype(jnp.int32)
    bandpass = draw_bandpass(jax.random.fold_in(key_list[4], 71), part)
    trial_delays = draw_trial_delays(jax.random.fold_in(key_list[4], 71), part)
    return {"voltages": voltages, "beam_delay": beam_delay, "bandpass": bandpass, "trial_delays": trial_delays}


two_pi = 2.0 * math.pi
phase_period = 4096

def forward_table():
    sample_index = jnp.arange(NT, dtype=jnp.int32)
    frequencies = jnp.arange(1, NF + 1, dtype=jnp.int32)
    angles = two_pi * (sample_index[:, None] * frequencies[None, :] % NT).astype(jnp.float32) / NT
    return jnp.stack([jnp.cos(angles), -jnp.sin(angles)], axis=1) / math.sqrt(NT)

def inverse_table():
    sample_index = jnp.arange(NT, dtype=jnp.int32)
    frequencies = jnp.arange(1, NF + 1, dtype=jnp.int32)
    angles = two_pi * (frequencies[:, None] * sample_index[None, :] % NT).astype(jnp.float32) / NT
    return (jnp.stack([jnp.cos(angles), -jnp.sin(angles)], axis=1) / math.sqrt(NT)).astype(jnp.bfloat16)

def weight_block(delays, channel):
    phases = delays * (channel + CHANNELS) % phase_period
    angles = two_pi * phases.astype(jnp.float32) / phase_period
    cosine = jnp.cos(angles)
    sine_part = jnp.sin(angles)
    upper_rows = jnp.concatenate([cosine, sine_part], axis=1)
    lower_rows = jnp.concatenate([-sine_part, cosine], axis=1)
    return (jnp.concatenate([upper_rows, lower_rows], axis=0) / math.sqrt(2 * ANTENNAS)).astype(jnp.bfloat16)

def channel_power(delays, channel, voltage, channel_gain):
    weights = weight_block(delays, channel)
    beam_count = delays.shape[0]
    beamformed = jnp.dot(weights, voltage.reshape(2 * voltage.shape[1], voltage.shape[2]), preferred_element_type=jnp.float32)
    squared = beamformed[:beam_count] ** 2 + beamformed[beam_count:] ** 2
    averaged = lax.optimization_barrier(jnp.mean(squared.reshape(beam_count, squared.shape[1] // INTEG, INTEG), axis=2))
    return averaged * channel_gain

def phasor_block(delays, frequency):
    angles = two_pi * (delays * frequency % NT).astype(jnp.float32) / NT
    cosine = jnp.cos(angles)
    sine_part = jnp.sin(angles)
    upper_rows = jnp.concatenate([cosine, -sine_part], axis=1)
    lower_rows = jnp.concatenate([sine_part, cosine], axis=1)
    return (jnp.concatenate([upper_rows, lower_rows], axis=0) / math.sqrt(CHANNELS)).astype(jnp.bfloat16)

def reference(voltages, beam_delay, bandpass, trial_delays):
    channels = jnp.arange(CHANNELS, dtype=jnp.int32)

    def one_channel(channel_entry):
        channel, voltage, channel_gain = channel_entry
        return channel_power(beam_delay, channel, voltage, channel_gain)
    power = lax.map(one_channel, (channels, voltages, bandpass))
    channel_mean = lax.optimization_barrier(jnp.sum(power, axis=0)) / CHANNELS
    spectra = jnp.einsum('cbt,tkf->kfcb', power - channel_mean, forward_table(), precision=lax.Precision.HIGHEST).astype(jnp.bfloat16)

    def one_frequency(freq_index):
        freq_slice = lax.dynamic_index_in_dim(spectra, freq_index, 1, keepdims=False)
        phasors = phasor_block(trial_delays, freq_index + 1)
        product = jnp.dot(phasors, freq_slice.reshape(2 * CHANNELS, BEAMS), preferred_element_type=jnp.float32)
        return product.astype(jnp.bfloat16).reshape(2, TRIALS, BEAMS)
    dedispersed_spectra = lax.map(one_frequency, jnp.arange(NF, dtype=jnp.int32))
    result = jnp.einsum('fkdb,fkt->dbt', dedispersed_spectra.astype(jnp.float32), inverse_table().astype(jnp.float32))
    return result.astype(jnp.bfloat16)
```

```python
import functools
import math

import numpy as np
import jax
import jax.numpy as jnp
from jax import lax
from jax.experimental import pallas as pl
from jax.experimental.pallas import tpu as pltpu
from jax.sharding import PartitionSpec as P

CHANNELS = 1024
ANTENNAS = 64
BEAMS = 256
NT = 512
INTEG = 4
TRIALS = 512
S_RAW = 2048
NF = 256
DEVICES = 64
LOCAL_CHANNELS = CHANNELS // DEVICES
LOCAL_TRIALS = TRIALS // DEVICES
LOCAL_FREQS = NF // DEVICES
PARTS_OF_F = 2 * LOCAL_FREQS
HALF = NT // 2
LANES = 128
PHASE_PERIOD = 4096
CHUNKS = 1

f32 = jnp.float32
bf16 = jnp.bfloat16


def _fit(function, terms, odd):
    nodes = np.cos(np.pi * (np.arange(400) + 0.5) / 400) * 0.5
    nodes = nodes[nodes > 0]
    squares = nodes * nodes
    target = function(np.pi * nodes)
    powers = np.stack([squares**k for k in range(terms)], axis=1)
    if odd:
        powers = powers * nodes[:, None]
    return [float(c) for c in np.linalg.lstsq(powers, target, rcond=None)[0]]


SIN_TERMS = _fit(np.sin, 6, True)
COS_TERMS = _fit(np.cos, 6, False)


def circle(turns, scale):
    part = turns - jnp.floor(turns + 0.5)
    square = part * part
    sine = jnp.full_like(square, SIN_TERMS[-1])
    for term in SIN_TERMS[-2::-1]:
        sine = sine * square + term
    sine = sine * part
    cosine = jnp.full_like(square, COS_TERMS[-1])
    for term in COS_TERMS[-2::-1]:
        cosine = cosine * square + term
    return scale - (2.0 * scale) * (sine * sine), (2.0 * scale) * (sine * cosine)


def split_halves(x):
    high = x.astype(bf16)
    return high, (x - high.astype(f32)).astype(bf16)


FINAL_STEPS = 8
contract_first = (((0,), (0,)), ((), ()))


def power_kernel(base_ref, gain_ref, delay_ref, v_ref, power_ref, sum_ref, squares_ref):
    step = pl.program_id(0)
    nb = delay_ref.shape[1]
    channel = (base_ref[0] + step + CHANNELS).astype(f32)
    turns = delay_ref[...].astype(f32) * (channel * (1.0 / PHASE_PERIOD))
    cosine, sine = circle(turns, 1.0 / math.sqrt(2 * ANTENNAS))
    upper = jnp.concatenate([cosine, -sine], axis=1)
    lower = jnp.concatenate([sine, cosine], axis=1)
    weights = jnp.concatenate([upper, lower], axis=0).astype(bf16)
    rows = 256
    for block in range(S_RAW // rows):
        beamformed = lax.dot_general(
            v_ref[0, :, block * rows : (block + 1) * rows], weights, contract_first, preferred_element_type=f32
        )
        squared = beamformed[:, :nb] ** 2 + beamformed[:, nb:] ** 2
        for g in range(nb // LANES):
            squares_ref[g, block * rows : (block + 1) * rows, :] = squared[:, g * LANES : (g + 1) * LANES]
    gain = gain_ref[step] * (1.0 / INTEG)
    for g in range(nb // LANES):
        lanes = slice(g * LANES, (g + 1) * LANES)
        ref = squares_ref.at[g]
        first, second = [
            sum(ref[pl.ds(start + j, HALF, stride=INTEG), :] for j in range(INTEG)) * gain
            for start in (0, HALF * INTEG)
        ]
        for parity, power in ((0, first - second), (1, first + second)):
            power_ref[0, parity, :, lanes] = power
            before = jnp.where(step == 0, 0.0, sum_ref[parity, :, lanes])
            sum_ref[parity, :, lanes] = before + power


def transform(high_ref, low_ref, parity, values):
    if parity == 1:
        values = values - jnp.mean(values, axis=0, keepdims=True)
    high, low = split_halves(values)
    spectra = jnp.dot(high_ref[parity], high, preferred_element_type=f32)
    spectra += jnp.dot(low_ref[parity], high, preferred_element_type=f32)
    return spectra + jnp.dot(high_ref[parity], low, preferred_element_type=f32)


def transform_kernel(power_ref, sum_ref, high_ref, low_ref, spectra_ref):
    step = pl.program_id(0)
    nb = sum_ref.shape[2]

    @pl.when(step == 0)
    def build_tables():
        for parity in range(2):
            row = lax.broadcasted_iota(jnp.int32, (HALF, HALF), 0)
            time = lax.broadcasted_iota(jnp.int32, (HALF, HALF), 1)
            freq = 8 * (row // 8) + 2 * ((row % 8) // 2) + 1 + parity
            turns = (freq.astype(f32) * time.astype(f32)) * (1.0 / NT)
            cosine, sine = circle(turns, 1.0 / math.sqrt(NT))
            high, low = split_halves(jnp.where(row % 2 == 0, cosine, -sine))
            high_ref[parity] = high
            low_ref[parity] = low

    for parity in range(2):
        values = power_ref[0, parity] - sum_ref[parity] * (1.0 / LOCAL_CHANNELS)
        spectra = transform(high_ref, low_ref, parity, values)
        for g in range(nb // LANES):
            spectra_ref.at[g][pl.ds(parity * HALF * LOCAL_CHANNELS + step, HALF, stride=LOCAL_CHANNELS), :] = (
                spectra[:, g * LANES : (g + 1) * LANES]
            )


def centre_kernel(sum_ref, mean_ref, high_ref, low_ref, spectra_ref, out_ref, shift_ref):
    step = pl.program_id(0)
    nb = sum_ref.shape[2]

    @pl.when(step == 0)
    def shifts():
        for parity in range(2):
            difference = sum_ref[parity] * (1.0 / LOCAL_CHANNELS) - mean_ref[parity]
            shift_ref[parity * HALF : (parity + 1) * HALF, :] = transform(high_ref, low_ref, parity, difference)

    dests = DEVICES // FINAL_STEPS
    rows = dests * PARTS_OF_F
    start = pl.multiple_of(step * rows, rows)
    for g in range(nb // LANES):
        lanes = slice(g * LANES, (g + 1) * LANES)
        shift = shift_ref[pl.ds(start, rows), lanes]
        for dest in range(dests):
            for j in range(PARTS_OF_F):
                row = dest * PARTS_OF_F + j
                values = spectra_ref[g, row * LOCAL_CHANNELS : (row + 1) * LOCAL_CHANNELS, :]
                out_ref[dest, j, :, lanes] = (values + shift[row : row + 1, :]).astype(bf16)


def phasor_kernel(base_ref, delays_ref, order_ref, cos_ref, sin_ref):
    delays = delays_ref[...].astype(f32)
    for j in range(LOCAL_FREQS):
        factor = (base_ref[0] + 2 * j).astype(f32) * (1.0 / NT)
        cosine, sine = circle(delays * factor, 1.0 / math.sqrt(CHANNELS))
        cos_ref[j] = cosine.astype(bf16)
        sin_ref[j] = sine.astype(bf16)


OUT_STEPS = 4


def dedisperse_kernel(values_ref, cos_ref, sin_ref, out_ref, acc_ref):
    step = pl.program_id(0)
    nb = values_ref.shape[3]
    groups = nb // LANES

    @pl.when(step < LOCAL_FREQS)
    def one_frequency():
        real_in = values_ref[:, 0].reshape(CHANNELS, nb)
        imaginary_in = values_ref[:, 1].reshape(CHANNELS, nb)
        dot = functools.partial(jnp.dot, preferred_element_type=f32)
        real = dot(cos_ref[0], real_in) - dot(sin_ref[0], imaginary_in)
        imaginary = dot(sin_ref[0], real_in) + dot(cos_ref[0], imaginary_in)
        for k, part in enumerate((real, imaginary)):
            for g in range(groups):
                acc_ref.at[g][pl.ds(2 * step + k, TRIALS, stride=PARTS_OF_F), :] = part[:, g * LANES : (g + 1) * LANES]

    @pl.when(step >= LOCAL_FREQS)
    def finish():
        dests = DEVICES // OUT_STEPS
        rows = dests * LOCAL_TRIALS * PARTS_OF_F
        start = pl.multiple_of((step - LOCAL_FREQS) * rows, rows)
        for g in range(groups):
            values = acc_ref[g, pl.ds(start, rows), :].reshape(dests, LOCAL_TRIALS, PARTS_OF_F, LANES)
            out_ref[:, :, :, g * LANES : (g + 1) * LANES] = values.astype(bf16)


def inverse_kernel(values_ref, table_ref, out_ref):
    nb = values_ref.shape[3]
    values = values_ref[:, 0].astype(f32).reshape(DEVICES * PARTS_OF_F, nb).astype(bf16)
    odd = lax.dot_general(values[:HALF], table_ref[0], contract_first, preferred_element_type=f32)
    even = lax.dot_general(values[HALF:], table_ref[1], contract_first, preferred_element_type=f32)
    out_ref[0, :, :HALF] = (even + odd).astype(bf16)
    out_ref[0, :, HALF:] = (even - odd).astype(bf16)


def inverse_into(values_ref, table_ref, filled_ref, out_ref):
    inverse_kernel(values_ref, table_ref, out_ref)


VMEM_LIMIT = 56 * 1024 * 1024
PARAMS = pltpu.CompilerParams(dimension_semantics=("arbitrary",), vmem_limit_bytes=VMEM_LIMIT)


def cost(flops, size):
    return pl.CostEstimate(flops=int(flops), bytes_accessed=int(size), transcendentals=0)


def whole(shape):
    return pl.BlockSpec(shape, lambda i: (0,) * len(shape))


def power_call(chunk, nb, base, bandpass, delays, voltages):
    smem = pl.BlockSpec(memory_space=pltpu.SMEM)
    return pl.pallas_call(
        power_kernel,
        grid=(LOCAL_CHANNELS,),
        in_specs=[
            smem,
            smem,
            pl.BlockSpec((ANTENNAS, nb), lambda i: (0, chunk)),
            pl.BlockSpec((1, 2 * ANTENNAS, S_RAW), lambda i: (i, 0, 0)),
        ],
        out_specs=[pl.BlockSpec((1, 2, HALF, nb), lambda i: (i, 0, 0, 0)), whole((2, HALF, nb))],
        out_shape=[
            jax.ShapeDtypeStruct((LOCAL_CHANNELS, 2, HALF, nb), f32),
            jax.ShapeDtypeStruct((2, HALF, nb), f32),
        ],
        scratch_shapes=[pltpu.VMEM((nb // LANES, S_RAW, LANES), f32)],
        compiler_params=PARAMS,
        cost_estimate=cost(9e9 * nb / BEAMS, 17e6),
        name="power",
    )(base, bandpass, delays, voltages)


def transform_call(nb, power, sums):
    groups = nb // LANES
    table = jax.ShapeDtypeStruct((2, HALF, HALF), bf16)
    return pl.pallas_call(
        transform_kernel,
        grid=(LOCAL_CHANNELS,),
        in_specs=[pl.BlockSpec((1, 2, HALF, nb), lambda i: (i, 0, 0, 0)), whole((2, HALF, nb))],
        out_specs=[
            whole((2, HALF, HALF)),
            whole((2, HALF, HALF)),
            whole((groups, NT * LOCAL_CHANNELS, LANES)),
        ],
        out_shape=[table, table, jax.ShapeDtypeStruct((groups, NT * LOCAL_CHANNELS, LANES), f32)],
        compiler_params=PARAMS,
        cost_estimate=cost(8e9 * nb / BEAMS, 17e6),
        name="transform",
    )(power, sums)


def centre_call(nb, sums, mean, high, low, spectra):
    groups = nb // LANES
    dests = DEVICES // FINAL_STEPS
    return pl.pallas_call(
        centre_kernel,
        grid=(FINAL_STEPS,),
        in_specs=[
            whole((2, HALF, nb)),
            whole((2, HALF, nb)),
            whole((2, HALF, HALF)),
            whole((2, HALF, HALF)),
            pl.BlockSpec((groups, dests * PARTS_OF_F * LOCAL_CHANNELS, LANES), lambda i: (0, i, 0)),
        ],
        out_specs=pl.BlockSpec((dests, PARTS_OF_F, LOCAL_CHANNELS, nb), lambda i: (i, 0, 0, 0)),
        out_shape=jax.ShapeDtypeStruct((DEVICES, PARTS_OF_F, LOCAL_CHANNELS, nb), bf16),
        scratch_shapes=[pltpu.VMEM((NT, nb), f32)],
        compiler_params=PARAMS,
        cost_estimate=cost(1e9 * nb / BEAMS, 13e6),
        name="centre",
    )(sums, mean, high, low, spectra)


def phasor_call(first_freq, trial_delays, order):
    rows = 32
    shape = jax.ShapeDtypeStruct((LOCAL_FREQS, TRIALS, CHANNELS), bf16)
    block = pl.BlockSpec((LOCAL_FREQS, rows, CHANNELS), lambda i: (0, i, 0))
    return pl.pallas_call(
        phasor_kernel,
        grid=(TRIALS // rows,),
        in_specs=[
            pl.BlockSpec(memory_space=pltpu.SMEM),
            pl.BlockSpec((rows, CHANNELS), lambda i: (i, 0)),
            pl.BlockSpec(memory_space=pl.ANY),
        ],
        out_specs=[block, block],
        out_shape=[shape, shape],
        compiler_params=PARAMS,
        cost_estimate=pl.CostEstimate(flops=8_000_000_000, bytes_accessed=10_000_000, transcendentals=0),
        name="phasors",
    )(first_freq, trial_delays, order)


def dedisperse_call(nb, received, cosines, sines):
    last = LOCAL_FREQS - 1
    dests = DEVICES // OUT_STEPS
    phasor_block = pl.BlockSpec((1, TRIALS, CHANNELS), lambda i: (jnp.minimum(i, last), 0, 0))
    return pl.pallas_call(
        dedisperse_kernel,
        grid=(LOCAL_FREQS + OUT_STEPS,),
        in_specs=[
            pl.BlockSpec((DEVICES, 2, LOCAL_CHANNELS, nb), lambda i: (0, jnp.minimum(i, last), 0, 0)),
            phasor_block,
            phasor_block,
        ],
        out_specs=pl.BlockSpec(
            (dests, LOCAL_TRIALS, PARTS_OF_F, nb), lambda i: (jnp.maximum(i - LOCAL_FREQS, 0), 0, 0, 0)
        ),
        out_shape=jax.ShapeDtypeStruct((DEVICES, LOCAL_TRIALS, PARTS_OF_F, nb), bf16),
        scratch_shapes=[pltpu.VMEM((nb // LANES, TRIALS * PARTS_OF_F, LANES), f32)],
        compiler_params=PARAMS,
        cost_estimate=cost(5e9 * nb / BEAMS, 15e6),
        name="dedisperse",
    )(received, cosines, sines)


def inverse_call(chunk, nb, received, table, filled):
    in_specs = [
        pl.BlockSpec((DEVICES, 1, LOCAL_TRIALS, nb), lambda i: (0, i, 0, 0)),
        pl.BlockSpec((2, HALF, HALF), lambda i: (0, 0, 0)),
    ]
    operands = [received, table]
    if filled is not None:
        in_specs.append(pl.BlockSpec(memory_space=pl.ANY))
        operands.append(filled)
    return pl.pallas_call(
        inverse_kernel if filled is None else inverse_into,
        grid=(LOCAL_TRIALS,),
        in_specs=in_specs,
        out_specs=pl.BlockSpec((1, nb, NT), lambda i: (i, chunk, 0)),
        out_shape=jax.ShapeDtypeStruct((LOCAL_TRIALS, BEAMS, NT), bf16),
        input_output_aliases={} if filled is None else {2: 0},
        compiler_params=PARAMS,
        cost_estimate=pl.CostEstimate(flops=1_000_000_000 * nb // BEAMS, bytes_accessed=4_000_000, transcendentals=0),
        name="inverse",
    )(*operands)


def shards(voltages, beam_delay, bandpass, trial_delays):
    position = lax.axis_index("ch").astype(jnp.int32)
    base = (position * LOCAL_CHANNELS).reshape(1)
    owners = DEVICES // 2
    first_freq = (8 * (position % owners) + 1 + position // owners).reshape(1)
    rows = voltages.reshape(LOCAL_CHANNELS, 2 * ANTENNAS, S_RAW)
    delays = beam_delay.T
    nb = BEAMS // CHUNKS
    exchange = functools.partial(lax.all_to_all, axis_name="ch", split_axis=0, concat_axis=0, tiled=True)
    powers = [power_call(chunk, nb, base, bandpass, delays, rows) for chunk in range(CHUNKS)]
    spectra, table = [], None
    for power, sums in powers:
        part = exchange(sums.reshape(DEVICES, PARTS_OF_F, nb))
        high, low, transformed = transform_call(nb, power, sums)
        part = jnp.sum(part, axis=0, keepdims=True) / CHANNELS
        mean = exchange(jnp.broadcast_to(part, (DEVICES, PARTS_OF_F, nb))).reshape(2, HALF, nb)
        spectra.append(exchange(centre_call(nb, sums, mean, high, low, transformed)))
        table = high
    cosines, sines = phasor_call(first_freq, trial_delays, table)
    trials = [exchange(dedisperse_call(nb, received, cosines, sines)) for received in spectra]
    result = None
    for chunk in range(CHUNKS):
        result = inverse_call(chunk, nb, trials[chunk], table, result)
    return result


def solution(mesh):
    return jax.shard_map(
        shards,
        mesh=mesh,
        in_specs=(P(("pt", "ch"), None, None, None), P("pt", None), P("ch"), P()),
        out_specs=P(("pt", "ch"), None, None),
        check_vma=False,
    )
```

```python
import functools
import math

import numpy as np
import jax
import jax.numpy as jnp
from jax import lax
from jax.experimental import pallas as pl
from jax.experimental.pallas import tpu as pltpu
from jax.sharding import PartitionSpec as P

CHANNELS = 1024
ANTENNAS = 64
BEAMS = 256
NT = 512
INTEG = 4
TRIALS = 512
S_RAW = 2048
NF = 256
DEVICES = 64
LOCAL_CHANNELS = CHANNELS // DEVICES
LOCAL_TRIALS = TRIALS // DEVICES
LOCAL_FREQS = NF // DEVICES
PARTS_OF_F = 2 * LOCAL_FREQS
HALF = NT // 2
LANES = 128
PHASE_PERIOD = 4096
CHUNKS = 1

f32 = jnp.float32
bf16 = jnp.bfloat16


def _fit(function, terms, odd):
    nodes = np.cos(np.pi * (np.arange(400) + 0.5) / 400) * 0.5
    nodes = nodes[nodes > 0]
    squares = nodes * nodes
    target = function(np.pi * nodes)
    powers = np.stack([squares**k for k in range(terms)], axis=1)
    if odd:
        powers = powers * nodes[:, None]
    return [float(c) for c in np.linalg.lstsq(powers, target, rcond=None)[0]]


SIN_TERMS = _fit(np.sin, 6, True)
COS_TERMS = _fit(np.cos, 6, False)


def circle(turns, scale):
    part = turns - jnp.floor(turns + 0.5)
    square = part * part
    sine = jnp.full_like(square, SIN_TERMS[-1])
    for term in SIN_TERMS[-2::-1]:
        sine = sine * square + term
    sine = sine * part
    cosine = jnp.full_like(square, COS_TERMS[-1])
    for term in COS_TERMS[-2::-1]:
        cosine = cosine * square + term
    return scale - (2.0 * scale) * (sine * sine), (2.0 * scale) * (sine * cosine)


def split_halves(x):
    high = x.astype(bf16)
    return high, (x - high.astype(f32)).astype(bf16)


FINAL_STEPS = 4
contract_first = (((0,), (0,)), ((), ()))


POWER_STEP = 4
TRANSFORM_STEP = 4


def power_kernel(base_ref, gain_ref, delay_ref, v_ref, order_ref, power_ref, sum_ref, squares_ref):
    step = pl.program_id(0)
    nb = delay_ref.shape[1]
    rows = 256

    @pl.when(step == 0)
    def clear():
        sum_ref[...] = jnp.zeros_like(sum_ref)

    for local in range(POWER_STEP):
        channel = step * POWER_STEP + local
        turns = delay_ref[...].astype(f32) * ((base_ref[0] + channel + CHANNELS).astype(f32) * (1.0 / PHASE_PERIOD))
        cosine, sine = circle(turns, 1.0 / math.sqrt(2 * ANTENNAS))
        upper = jnp.concatenate([cosine, -sine], axis=1)
        lower = jnp.concatenate([sine, cosine], axis=1)
        weights = jnp.concatenate([upper, lower], axis=0).astype(bf16)
        slot = local % 2
        for block in range(S_RAW // rows):
            beamformed = lax.dot_general(
                v_ref[local, :, block * rows : (block + 1) * rows], weights, contract_first, preferred_element_type=f32
            )
            squared = beamformed[:, :nb] ** 2 + beamformed[:, nb:] ** 2
            for g in range(nb // LANES):
                squares_ref[slot, g, block * rows : (block + 1) * rows, :] = squared[:, g * LANES : (g + 1) * LANES]
        gain = gain_ref[channel] * (1.0 / INTEG)
        for g in range(nb // LANES):
            lanes = slice(g * LANES, (g + 1) * LANES)
            ref = squares_ref.at[slot, g]
            first, second = [
                sum(ref[pl.ds(start + j, HALF, stride=INTEG), :] for j in range(INTEG)) * gain
                for start in (0, HALF * INTEG)
            ]
            for parity, power in ((0, first - second), (1, first + second)):
                power_ref[local, parity, :, lanes] = power
                sum_ref[parity, :, lanes] += power


def transform(table_ref, parity, values):
    if parity == 1:
        values = values - jnp.mean(values, axis=0, keepdims=True)
    high, low = split_halves(values)
    return jnp.dot(table_ref[parity], jnp.concatenate([high, high, low], axis=0), preferred_element_type=f32)


def transform_kernel(power_ref, sum_ref, table_ref, spectra_ref):
    step = pl.program_id(0)
    nb = sum_ref.shape[2]

    @pl.when(step == 0)
    def build_tables():
        for parity in range(2):
            row = lax.broadcasted_iota(jnp.int32, (HALF, HALF), 0)
            time = lax.broadcasted_iota(jnp.int32, (HALF, HALF), 1)
            freq = 8 * (row // 8) + 2 * ((row % 8) // 2) + 1 + parity
            turns = (freq.astype(f32) * time.astype(f32)) * (1.0 / NT)
            cosine, sine = circle(turns, 1.0 / math.sqrt(NT))
            high, low = split_halves(jnp.where(row % 2 == 0, cosine, -sine))
            table_ref[parity, :, :HALF] = high
            table_ref[parity, :, HALF : 2 * HALF] = low
            table_ref[parity, :, 2 * HALF :] = high

    for local in range(TRANSFORM_STEP):
        for parity in range(2):
            values = power_ref[local, parity] - sum_ref[parity] * (1.0 / LOCAL_CHANNELS)
            spectra = transform(table_ref, parity, values)
            start = parity * HALF * LOCAL_CHANNELS + step * TRANSFORM_STEP + local
            for g in range(nb // LANES):
                spectra_ref.at[g][pl.ds(start, HALF, stride=LOCAL_CHANNELS), :] = (
                    spectra[:, g * LANES : (g + 1) * LANES]
                )


def centre_kernel(sum_ref, mean_ref, table_ref, spectra_ref, out_ref, shift_ref):
    step = pl.program_id(0)
    nb = sum_ref.shape[2]

    @pl.when(step == 0)
    def shifts():
        for parity in range(2):
            difference = sum_ref[parity] * (1.0 / LOCAL_CHANNELS) - mean_ref[parity]
            shift_ref[parity * HALF : (parity + 1) * HALF, :] = transform(table_ref, parity, difference)

    dests = DEVICES // FINAL_STEPS
    rows = dests * PARTS_OF_F
    start = pl.multiple_of(step * rows, rows)
    for g in range(nb // LANES):
        lanes = slice(g * LANES, (g + 1) * LANES)
        shift = shift_ref[pl.ds(start, rows), lanes]
        for dest in range(dests):
            for j in range(PARTS_OF_F):
                row = dest * PARTS_OF_F + j
                values = spectra_ref[g, row * LOCAL_CHANNELS : (row + 1) * LOCAL_CHANNELS, :]
                out_ref[dest, j, :, lanes] = (values + shift[row : row + 1, :]).astype(bf16)


PHASOR_ROWS = 128
PHASOR_STEPS = TRIALS // PHASOR_ROWS


def phasor_kernel(plan_ref, delays_ref, *refs):
    cos_ref, sin_ref = refs[-2:]

    @pl.when(plan_ref[1] != 0)
    def make():
        delays = delays_ref[...].astype(f32)
        for j in range(LOCAL_FREQS):
            factor = (plan_ref[0] + 2 * j).astype(f32) * (1.0 / NT)
            cosine, sine = circle(delays * factor, 1.0 / math.sqrt(CHANNELS))
            cos_ref[j] = cosine.astype(bf16)
            sin_ref[j] = sine.astype(bf16)

    if len(refs) > 2:

        @pl.when((plan_ref[1] == 0) & (pl.program_id(0) == 0))
        def keep():
            cos_ref[...] = refs[0][...]
            sin_ref[...] = refs[1][...]


OUT_STEPS = 2


def dedisperse_kernel(values_ref, cos_ref, sin_ref, out_ref, acc_ref):
    step = pl.program_id(0)
    nb = values_ref.shape[3]
    groups = nb // LANES

    @pl.when(step < LOCAL_FREQS)
    def one_frequency():
        real_in = values_ref[:, 0].reshape(CHANNELS, nb)
        imaginary_in = values_ref[:, 1].reshape(CHANNELS, nb)
        dot = functools.partial(jnp.dot, preferred_element_type=f32)
        real = dot(cos_ref[0], real_in) - dot(sin_ref[0], imaginary_in)
        imaginary = dot(sin_ref[0], real_in) + dot(cos_ref[0], imaginary_in)
        for k, part in enumerate((real, imaginary)):
            for g in range(groups):
                acc_ref.at[g][pl.ds(2 * step + k, TRIALS, stride=PARTS_OF_F), :] = part[:, g * LANES : (g + 1) * LANES]

    @pl.when(step >= LOCAL_FREQS)
    def finish():
        dests = DEVICES // OUT_STEPS
        rows = dests * LOCAL_TRIALS * PARTS_OF_F
        start = pl.multiple_of((step - LOCAL_FREQS) * rows, rows)
        for g in range(groups):
            values = acc_ref[g, pl.ds(start, rows), :].reshape(dests, LOCAL_TRIALS, PARTS_OF_F, LANES)
            out_ref[:, :, :, g * LANES : (g + 1) * LANES] = values.astype(bf16)


INVERSE_STEP = 2


def inverse_kernel(values_ref, table_ref, out_ref):
    nb = values_ref.shape[3]
    for trial in range(INVERSE_STEP):
        values = values_ref[:, trial].astype(f32).reshape(DEVICES * PARTS_OF_F, nb).astype(bf16)
        odd = lax.dot_general(values[:HALF], table_ref[0], contract_first, preferred_element_type=f32)
        even = lax.dot_general(values[HALF:], table_ref[1], contract_first, preferred_element_type=f32)
        out_ref[trial, :, :HALF] = (even + odd).astype(bf16)
        out_ref[trial, :, HALF:] = (even - odd).astype(bf16)


def inverse_into(values_ref, table_ref, filled_ref, out_ref):
    inverse_kernel(values_ref, table_ref, out_ref)


VMEM_LIMIT = 56 * 1024 * 1024
PARAMS = pltpu.CompilerParams(dimension_semantics=("arbitrary",), vmem_limit_bytes=VMEM_LIMIT)


def cost(flops, size):
    return pl.CostEstimate(flops=int(flops), bytes_accessed=int(size), transcendentals=0)


def whole(shape):
    return pl.BlockSpec(shape, lambda i: (0,) * len(shape))


def power_call(chunk, nb, base, bandpass, delays, voltages, order):
    smem = pl.BlockSpec(memory_space=pltpu.SMEM)
    return pl.pallas_call(
        power_kernel,
        grid=(LOCAL_CHANNELS // POWER_STEP,),
        in_specs=[
            smem,
            smem,
            pl.BlockSpec((ANTENNAS, nb), lambda i: (0, chunk)),
            pl.BlockSpec((POWER_STEP, 2 * ANTENNAS, S_RAW), lambda i: (i, 0, 0)),
            pl.BlockSpec(memory_space=pl.ANY),
        ],
        out_specs=[pl.BlockSpec((POWER_STEP, 2, HALF, nb), lambda i: (i, 0, 0, 0)), whole((2, HALF, nb))],
        out_shape=[
            jax.ShapeDtypeStruct((LOCAL_CHANNELS, 2, HALF, nb), f32),
            jax.ShapeDtypeStruct((2, HALF, nb), f32),
        ],
        scratch_shapes=[pltpu.VMEM((2, nb // LANES, S_RAW, LANES), f32)],
        compiler_params=PARAMS,
        cost_estimate=cost(9e9 * nb / BEAMS, 17e6),
        name="power",
    )(base, bandpass, delays, voltages, order)


def transform_call(nb, power, sums):
    groups = nb // LANES
    table = jax.ShapeDtypeStruct((2, HALF, 3 * HALF), bf16)
    return pl.pallas_call(
        transform_kernel,
        grid=(LOCAL_CHANNELS // TRANSFORM_STEP,),
        in_specs=[pl.BlockSpec((TRANSFORM_STEP, 2, HALF, nb), lambda i: (i, 0, 0, 0)), whole((2, HALF, nb))],
        out_specs=[
            whole((2, HALF, 3 * HALF)),
            whole((groups, NT * LOCAL_CHANNELS, LANES)),
        ],
        out_shape=[table, jax.ShapeDtypeStruct((groups, NT * LOCAL_CHANNELS, LANES), f32)],
        compiler_params=PARAMS,
        cost_estimate=cost(8e9 * nb / BEAMS, 17e6),
        name="transform",
    )(power, sums)


def centre_call(nb, sums, mean, table, spectra):
    groups = nb // LANES
    dests = DEVICES // FINAL_STEPS
    return pl.pallas_call(
        centre_kernel,
        grid=(FINAL_STEPS,),
        in_specs=[
            whole((2, HALF, nb)),
            whole((2, HALF, nb)),
            whole((2, HALF, 3 * HALF)),
            pl.BlockSpec((groups, dests * PARTS_OF_F * LOCAL_CHANNELS, LANES), lambda i: (0, i, 0)),
        ],
        out_specs=pl.BlockSpec((dests, PARTS_OF_F, LOCAL_CHANNELS, nb), lambda i: (i, 0, 0, 0)),
        out_shape=jax.ShapeDtypeStruct((DEVICES, PARTS_OF_F, LOCAL_CHANNELS, nb), bf16),
        scratch_shapes=[pltpu.VMEM((NT, nb), f32)],
        compiler_params=PARAMS,
        cost_estimate=cost(1e9 * nb / BEAMS, 13e6),
        name="centre",
    )(sums, mean, table, spectra)


def phasor_call(active, first_freq, trial_delays, earlier=(), order=None):
    shape = jax.ShapeDtypeStruct((LOCAL_FREQS, TRIALS, CHANNELS), bf16)
    block = pl.BlockSpec((LOCAL_FREQS, PHASOR_ROWS, CHANNELS), lambda i, plan: (0, i * plan[1], 0))
    first = pl.BlockSpec((LOCAL_FREQS, PHASOR_ROWS, CHANNELS), lambda i, plan: (0, 0, 0))
    operands = [trial_delays, *earlier] + ([] if order is None else [order])
    in_specs = [pl.BlockSpec((PHASOR_ROWS, CHANNELS), lambda i, plan: (i * plan[1], 0))]
    in_specs += [first] * len(earlier) + [pl.BlockSpec(memory_space=pl.ANY)] * (order is not None)
    return pl.pallas_call(
        phasor_kernel,
        grid_spec=pltpu.PrefetchScalarGridSpec(
            num_scalar_prefetch=1, grid=(PHASOR_STEPS,), in_specs=in_specs, out_specs=[block, block]
        ),
        out_shape=[shape, shape],
        input_output_aliases={2: 0, 3: 1} if earlier else {},
        compiler_params=PARAMS,
        cost_estimate=cost(8e9, 10e6),
        name="phasors",
    )(jnp.stack([first_freq, active]), *operands)


def dedisperse_call(nb, received, cosines, sines):
    last = LOCAL_FREQS - 1
    dests = DEVICES // OUT_STEPS
    phasor_block = pl.BlockSpec((1, TRIALS, CHANNELS), lambda i: (jnp.minimum(i, last), 0, 0))
    return pl.pallas_call(
        dedisperse_kernel,
        grid=(LOCAL_FREQS + OUT_STEPS,),
        in_specs=[
            pl.BlockSpec((DEVICES, 2, LOCAL_CHANNELS, nb), lambda i: (0, jnp.minimum(i, last), 0, 0)),
            phasor_block,
            phasor_block,
        ],
        out_specs=pl.BlockSpec(
            (dests, LOCAL_TRIALS, PARTS_OF_F, nb), lambda i: (jnp.maximum(i - LOCAL_FREQS, 0), 0, 0, 0)
        ),
        out_shape=jax.ShapeDtypeStruct((DEVICES, LOCAL_TRIALS, PARTS_OF_F, nb), bf16),
        scratch_shapes=[pltpu.VMEM((nb // LANES, TRIALS * PARTS_OF_F, LANES), f32)],
        compiler_params=PARAMS,
        cost_estimate=cost(5e9 * nb / BEAMS, 15e6),
        name="dedisperse",
    )(received, cosines, sines)


def inverse_call(chunk, nb, received, table, filled):
    in_specs = [
        pl.BlockSpec((DEVICES, INVERSE_STEP, LOCAL_TRIALS, nb), lambda i: (0, i, 0, 0)),
        pl.BlockSpec((2, HALF, HALF), lambda i: (0, 0, 0)),
    ]
    operands = [received, table]
    if filled is not None:
        in_specs.append(pl.BlockSpec(memory_space=pl.ANY))
        operands.append(filled)
    return pl.pallas_call(
        inverse_kernel if filled is None else inverse_into,
        grid=(LOCAL_TRIALS // INVERSE_STEP,),
        in_specs=in_specs,
        out_specs=pl.BlockSpec((INVERSE_STEP, nb, NT), lambda i: (i, chunk, 0)),
        out_shape=jax.ShapeDtypeStruct((LOCAL_TRIALS, BEAMS, NT), bf16),
        input_output_aliases={} if filled is None else {2: 0},
        compiler_params=PARAMS,
        cost_estimate=pl.CostEstimate(flops=1_000_000_000 * nb // BEAMS, bytes_accessed=4_000_000, transcendentals=0),
        name="inverse",
    )(*operands)


def shards(voltages, beam_delay, bandpass, trial_delays):
    position = lax.axis_index("ch").astype(jnp.int32)
    base = (position * LOCAL_CHANNELS).reshape(1)
    owners = DEVICES // 2
    first_freq = 8 * (position % owners) + 1 + position // owners
    rows = voltages.reshape(LOCAL_CHANNELS, 2 * ANTENNAS, S_RAW)
    delays = beam_delay.T
    nb = BEAMS // CHUNKS
    exchange = functools.partial(lax.all_to_all, axis_name="ch", split_axis=0, concat_axis=0, tiled=True)
    early = lax.axis_index("pt").astype(jnp.int32) % 2
    phasors = phasor_call(early, first_freq, trial_delays)
    powers = [power_call(chunk, nb, base, bandpass, delays, rows, phasors[0]) for chunk in range(CHUNKS)]
    spectra = []
    for power, sums in powers:
        part = exchange(sums.reshape(DEVICES, PARTS_OF_F, nb))
        table, transformed = transform_call(nb, power, sums)
        part = jnp.sum(part, axis=0, keepdims=True) / CHANNELS
        mean = exchange(jnp.broadcast_to(part, (DEVICES, PARTS_OF_F, nb))).reshape(2, HALF, nb)
        sent = centre_call(nb, sums, mean, table, transformed)
        spectra.append(exchange(sent))
    cosines, sines = phasor_call(1 - early, first_freq, trial_delays, phasors, sent)
    trials = [exchange(dedisperse_call(nb, received, cosines, sines)) for received in spectra]
    result = None
    for chunk in range(CHUNKS):
        result = inverse_call(chunk, nb, trials[chunk], table, result)
    return result


def solution(mesh):
    return jax.shard_map(
        shards,
        mesh=mesh,
        in_specs=(P(("pt", "ch"), None, None, None), P("pt", None), P("ch"), P()),
        out_specs=P(("pt", "ch"), None, None),
        check_vma=False,
    )
```
